32 devices in a mesh: groups: 2 (over x), beam: 4 (over z), ctx: 4 (over y, core).
Axes of the slice: x: 2, y: 2, z: 4, core: 2. Of those that a mesh axis runs over, the one named last changes fastest.
Arguments:
- queries: bfloat16 [8, 16384], P(('groups', 'beam'), 'ctx'), parts along dimension 0
- new_keys: bfloat16 [8, 1024], P(('groups', 'beam')), parts along dimension 0, may hold values from -16 to 16
- new_values: bfloat16 [8, 1024], P(('groups', 'beam')), parts along dimension 0, may hold values from -9 to 9
- cache_keys: bfloat16 [8, 2048, 8, 128], P(('groups', 'beam'), 'ctx'), parts along dimension 0
- cache_values: bfloat16 [8, 2048, 8, 128], P(('groups', 'beam'), 'ctx'), parts along dimension 0, may hold values from -6 to 6
- parents: int32 [8], P('groups'), parts along dimension 0, may hold values from 0 to 3
- lengths: int32 [8], P('groups'), parts along dimension 0, may hold values from 8 to 16, as said below
- out_weight: bfloat16 [16384, 16384], P('ctx', 'beam'), may hold values from -0.046875 to 0.046875
Outputs:
- projected: bfloat16 [8, 16384], P('groups', ('beam', 'ctx')), parts along dimension 0
The draws below stay inside these ranges and needn't reach their ends.
There are 2 independent parts, one for each index of `groups`. The reference program is written for one: setup_inputs(seed, part) draws one part's arguments, and reference() takes and returns one part's arrays. A program takes and returns all parts, laid end to end along the dimension named above; an argument that names none is the same for every part. Nothing has to cross between parts.
Inputs may be any that keep to these rules, and one draw needn't show every extreme that they name: `lengths`: each previous beam holds at least half of its 16 spans; in every draw some beam is full.
All inputs are finite; a program needn't handle non-finite values.
Results may differ from the reference program's by a relative error of at most 0.012.
Values may be sent and summed in bfloat16 or wider, within the bound.
No kernel may reach another device: no remote copies, remote signals or barrier semaphores. Data moves between devices by JAX's collectives and lax.ppermute only.
A program may use at most 64 MiB of HBM per device.

```python
import math
import jax
import jax.numpy as jnp
import numpy as np
from jax import lax

D = 16384
H = 128
KVH = 8
HD = 128
SPAN = 128
BEAMS = 4
CONTEXT = 2048
SPANS = 16


def draw_queries(key, part):
    log_scale = jax.random.uniform(jax.random.fold_in(key, 4), (BEAMS, H, 1), jnp.float32, -2.302585, 2.302585)
    entries = jnp.clip(jax.random.normal(jax.random.fold_in(key, 1), (BEAMS, H, HD), jnp.float32), -4.0, 4.0)
    drawn = entries * jnp.exp(log_scale)
    return drawn.reshape(BEAMS, H * HD).astype(jnp.bfloat16)


def draw_cache_keys(key, part):
    drawn = jnp.clip(2.0 * jax.random.normal(jax.random.fold_in(key, 11), (BEAMS, CONTEXT, KVH, HD), jnp.float32), -12.0, 12.0)
    return drawn.astype(jnp.bfloat16)


def draw_lengths(key, part):
    drawn = jax.random.randint(jax.random.fold_in(key, 5), (BEAMS,), SPANS // 2, SPANS + 1)
    fullest = jax.random.randint(jax.random.fold_in(key, 6), (), 0, BEAMS)
    return jnp.where(jnp.arange(BEAMS, dtype=jnp.int32) == fullest, SPANS, drawn).astype(jnp.int32)


def with_ends(entries, key, smallest, high):
    longest = entries.shape.index(max(entries.shape))
    spots = []
    for shift in (0, 1):
        where = [jax.random.randint(jax.random.fold_in(key, axis), (), 0, length) for axis, length in enumerate(entries.shape)]
        where[longest] = (where[longest] + shift) % entries.shape[longest]
        spots.append(tuple(where))
    return entries.at[spots[0]].set(smallest).at[spots[1]].set(high)


def block_scale(own_key, extent, shards, least, high):
    level, own = 1.0, jax.random.fold_in(own_key, 6)
    for dim, shards_of in shards:
        steps = jnp.exp(jax.random.uniform(jax.random.fold_in(own, dim), (shards_of,), jnp.float32, least / len(shards), high / len(shards)))
        level = level * jnp.repeat(steps, extent[dim] // shards_of).reshape([-1 if axis == dim else 1 for axis in range(len(extent))])
    return level


def cumulative_ranks(amount, lean):
    weights = [(1 << 20) // math.isqrt(grade ** lean) + 1 for grade in range(1, amount + 1)]
    deviation = 1 + sum(weights) // (1 << 30)
    return np.cumsum(np.array([max(1, weight // deviation) for weight in weights]))


def skewed_ids(key, extent, amount, lean):
    grid = cumulative_ranks(amount, lean)
    ticket = jax.random.randint(jax.random.fold_in(key, 1), extent, 0, int(grid[amount - 1]))
    standing = jnp.searchsorted(jnp.asarray(grid, jnp.int32), ticket, side="right")
    return jax.random.permutation(jax.random.fold_in(key, 2), amount)[standing].astype(jnp.int32)


def gaussian(own_key, dims, spread, limit, split=(), kind=jnp.bfloat16):
    factor_of = block_scale(own_key, dims, split, -0.22, 0.18) if split else 1.0
    values = jax.random.normal(own_key, dims, jnp.float32) * spread * factor_of
    return jnp.minimum(jnp.maximum(values, -limit), limit).astype(kind)


def setup_inputs(seed: int = 0, part: int = 0) -> dict:
    key_list = jax.random.split(jax.random.key(seed), 9)
    own_keys = jax.random.split(jax.random.fold_in(key_list[8], part), 9)
    return {
        "queries": draw_queries(jax.random.fold_in(jax.random.fold_in(key_list[8], part), 71), part),
        "new_keys": gaussian(own_keys[1], (BEAMS, KVH * HD), 4.0, 16.0, ((0, 4),)),
        "new_values": gaussian(own_keys[2], (BEAMS, KVH * HD), 1.5, 9.0, ((0, 4),)),
        "cache_keys": draw_cache_keys(jax.random.fold_in(jax.random.fold_in(key_list[8], part), 71), part),
        "cache_values": gaussian(own_keys[4], (BEAMS, CONTEXT, KVH, HD), 1.0, 6.0, ((0, 4), (1, 4))),
        "parents": with_ends(skewed_ids(own_keys[5], (BEAMS,), BEAMS, 2), jax.random.fold_in(own_keys[5], 3), 0, BEAMS - 1).astype(jnp.int32),
        "lengths": draw_lengths(jax.random.fold_in(jax.random.fold_in(key_list[8], part), 71), part),
        "out_weight": gaussian(key_list[7], (H * HD, D), (H * HD) ** -0.5, 0.046875, ((0, 4), (1, 4))),
    }


MASKED = -1e+30

def attend_child(query, new_key, new_value, parent_keys, parent_values, length):
    group_size = H // KVH
    scale = 1.0 / math.sqrt(HD)
    grouped = query.astype(jnp.float32).reshape(KVH, group_size, HD)
    scores = jnp.einsum('kgd,tkd->kgt', grouped, parent_keys.astype(jnp.float32)) * scale
    usable = jnp.arange(CONTEXT, dtype=jnp.int32) < length * SPAN
    scores = jnp.where(usable[None, None, :], scores, MASKED)
    own_score = jnp.einsum('kgd,kd->kg', grouped, new_key.astype(jnp.float32).reshape(KVH, HD)) * scale
    peak = jnp.maximum(lax.optimization_barrier(jnp.max(scores, axis=-1)), own_score)
    weights = jnp.where(usable[None, None, :], jnp.exp(scores - peak[..., None]), 0.0)
    own_weight = jnp.exp(own_score - peak)
    weight_sum = lax.optimization_barrier(jnp.sum(weights, axis=-1)) + own_weight
    rounded = lax.optimization_barrier(weights.astype(jnp.bfloat16)).astype(jnp.float32)
    own_rounded = lax.optimization_barrier(own_weight.astype(jnp.bfloat16)).astype(jnp.float32)
    blended = jnp.einsum('kgt,tkd->kgd', rounded, parent_values.astype(jnp.float32))
    blended = blended + own_rounded[..., None] * new_value.astype(jnp.float32).reshape(KVH, 1, HD)
    return (blended / weight_sum[..., None]).reshape(H * HD).astype(jnp.bfloat16)

def reference(queries, new_keys, new_values, cache_keys, cache_values, parents, lengths, out_weight):

    def per_child(child):
        parent = parents[child]
        return attend_child(queries[child], new_keys[child], new_values[child], cache_keys[parent], cache_values[parent], lengths[parent])
    attended = lax.map(per_child, jnp.arange(BEAMS, dtype=jnp.int32))
    return jnp.dot(attended, out_weight, preferred_element_type=jnp.float32).astype(jnp.bfloat16)
```

```python
import math

import jax
import jax.numpy as jnp
from jax import lax
from jax.experimental import pallas as pl
from jax.experimental.pallas import tpu as pltpu
from jax.sharding import PartitionSpec as P

H = 128
KVH = 8
HD = 128
SPAN = 128
GROUP = H // KVH

MASKED = -1e30
SCALE = 1.0 / math.sqrt(HD)

BF = jnp.bfloat16
F32 = jnp.float32
VMEM = pl.BlockSpec(memory_space=pltpu.VMEM)
SMEM = pl.BlockSpec(memory_space=pltpu.SMEM)


def params(mib):
    return pltpu.CompilerParams(vmem_limit_bytes=mib << 20)


def cost(flops, moved):
    return pl.CostEstimate(flops=flops, bytes_accessed=moved, transcendentals=0)


def partner(array, axis, k):
    length = lax.axis_size(axis)
    return lax.ppermute(array, axis, [(i, i ^ k) for i in range(length)])


def pack_kernel(heads, kv_count, q_ref, k_ref, v_ref, out_ref, rows):
    start = lax.axis_index("ctx") * heads // GROUP
    rows[...] = jnp.zeros_like(rows)
    for h in range(heads):
        rows[h : h + 1, :] = q_ref[:, h * HD : (h + 1) * HD].astype(F32)
    for r in range(kv_count):
        here = pl.ds(pl.multiple_of((start + r) * HD, HD), HD)
        rows[heads + r : heads + r + 1, :] = k_ref[:, here].astype(F32)
        rows[heads + kv_count + r : heads + kv_count + r + 1, :] = v_ref[:, here].astype(F32)
    out_ref[...] = rows[...].astype(BF)


def split3(x):
    a = x.astype(BF)
    rest = x - a.astype(F32)
    b = rest.astype(BF)
    c = (rest - b.astype(F32)).astype(BF)
    return a, b, c


def eye(rows):
    shape = (rows, HD)
    return lax.broadcasted_iota(jnp.int32, shape, 0) == lax.broadcasted_iota(jnp.int32, shape, 1)


def attend_kernel(ctx_count, beams, heads, kv_count, per_kv, tokens, *refs):
    lengths, refs = refs[0], refs[1:]
    stacks, (kt, vt), outs = refs[:ctx_count], refs[ctx_count : ctx_count + 2], refs[ctx_count + 2 :]
    c = lax.axis_index("ctx")
    limit = lengths[lax.axis_index("beam")] * SPAN - c * tokens
    rows = beams * per_kv
    keep = lax.broadcasted_iota(jnp.int32, (rows, tokens), 1) < limit
    for k in range(ctx_count):
        first = (c ^ k) * heads // GROUP
        lses = []
        for r in range(kv_count):
            q = stacks[k][:, r * per_kv : (r + 1) * per_kv, :].astype(F32)
            q = q.reshape(rows, HD).astype(BF)
            s = lax.dot_general(q, kt[first + r], (((1,), (1,)), ((), ())), preferred_element_type=F32)
            s = jnp.where(keep, s * SCALE, MASKED)
            peak = jnp.max(s, axis=-1, keepdims=True)
            w = jnp.where(keep, jnp.exp(s - peak), 0.0)
            total = jnp.sum(w, axis=-1, keepdims=True)
            o = jnp.dot(w.astype(BF), vt[first + r], preferred_element_type=F32)
            some = total > 0.0
            safe = jnp.where(some, total, 1.0)
            outs[k][r * rows : (r + 1) * rows, :] = (o / safe).astype(BF)
            lses.append(jnp.where(some, peak + jnp.log(safe), MASKED))
        lse = jnp.concatenate(lses, axis=0) if kv_count > 1 else lses[0]
        count = kv_count * rows
        line = jnp.sum(jnp.where(eye(count), lse, 0.0), axis=0, keepdims=True)
        parts = [p.astype(F32) for p in split3(line)]
        which = lax.broadcasted_iota(jnp.int32, (16, HD), 0)
        stats = jnp.where(which == 0, parts[0], jnp.where(which == 1, parts[1], jnp.where(which == 2, parts[2], 0.0)))
        outs[k][count : count + 16, :] = stats.astype(BF)


def merge_kernel(ctx_count, beams, heads, kv_count, per_kv, *refs):
    stack, states, out_ref = refs[0], refs[1 : 1 + ctx_count], refs[1 + ctx_count]
    b = lax.axis_index("beam")
    rows = beams * per_kv
    count = kv_count * rows
    diagonal = eye(count)
    own, value = [], []
    for r in range(kv_count):
        q = stack[:, r * per_kv : (r + 1) * per_kv, :].astype(F32)
        key = stack[:, heads + r : heads + r + 1, :].astype(F32)
        own.append(jnp.sum(q * key, axis=-1, keepdims=True).reshape(rows, 1) * SCALE)
        v = stack[:, heads + kv_count + r : heads + kv_count + r + 1, :].astype(F32)
        value.append(jnp.broadcast_to(v, (beams, per_kv, HD)).reshape(rows, HD))
    own = jnp.concatenate(own, axis=0) if kv_count > 1 else own[0]
    value = jnp.concatenate(value, axis=0) if kv_count > 1 else value[0]
    lses = []
    for k in range(ctx_count):
        line = states[k][count : count + 16, :].astype(F32)
        line = line[0:1] + line[1:2] + line[2:3]
        lses.append(jnp.sum(jnp.where(diagonal, line, 0.0), axis=-1, keepdims=True))
    peak = own
    for lse in lses:
        peak = jnp.maximum(peak, lse)
    weight = jnp.exp(own - peak)
    total = weight
    blended = weight * value
    for k in range(ctx_count):
        weight = jnp.exp(lses[k] - peak)
        total = total + weight
        blended = blended + weight * states[k][0:count, :].astype(F32)
    result = (blended / total).astype(BF)
    for r in range(kv_count):
        for i in range(beams):
            at = r * rows + i * per_kv
            out_ref[b ^ i, r * per_kv : (r + 1) * per_kv, :] = result[at : at + per_kv, :]


def project_kernel(ctx_count, beams, heads, *refs):
    parents, rows_of, weight = refs[0], refs[1 : 1 + beams], refs[1 + beams]
    outs, (laid, wide) = refs[2 + beams : 2 + beams + ctx_count], refs[2 + beams + ctx_count :]
    b = lax.axis_index("beam")
    c = lax.axis_index("ctx")
    laid[...] = jnp.zeros_like(laid)
    for i in range(beams):
        source = parents[i] ^ b
        row = rows_of[0][i].astype(F32)
        for k in range(1, beams):
            row = jnp.where(source == k, rows_of[k][i].astype(F32), row)
        laid[i * heads : (i + 1) * heads, :] = row
    for h in range(heads):
        wide[:, h * HD : (h + 1) * HD] = laid[pl.ds(h, 8, stride=heads), :].astype(BF)
    columns = weight.shape[1] // ctx_count
    step = min(512, columns)
    for k in range(ctx_count):
        for j in range(columns // step):
            at = pl.multiple_of((c ^ k) * columns + j * step, 128)
            part = jnp.dot(wide[...], weight[:, pl.ds(at, step)], preferred_element_type=F32)
            outs[k][:, j * step : (j + 1) * step] = part[:beams]


def per_device(
    queries, new_keys, new_values, cache_keys, cache_values, parents, lengths, out_weight
):
    ctx_count = lax.axis_size("ctx")
    beams = lax.axis_size("beam")
    heads = queries.shape[1] // HD
    tokens = cache_keys.shape[1]
    kv_count = max(1, heads // GROUP)
    per_kv = min(heads, GROUP)
    packet_rows = -(-(heads + 2 * kv_count) // 16) * 16
    count = beams * heads

    packet = pl.pallas_call(
        lambda *refs: pack_kernel(heads, kv_count, *refs),
        out_shape=jax.ShapeDtypeStruct((packet_rows, HD), BF),
        in_specs=[VMEM] * 3,
        out_specs=VMEM,
        scratch_shapes=[pltpu.VMEM((packet_rows, HD), F32)],
        compiler_params=params(4),
        name="pack",
    )(queries, new_keys, new_values)
    kt = jnp.transpose(cache_keys[0], (1, 0, 2))
    vt = jnp.transpose(cache_values[0], (1, 0, 2))
    stack = jnp.stack([packet] + [partner(packet, "beam", k) for k in range(1, beams)])
    stacks = [stack] + [partner(stack, "ctx", k) for k in range(1, ctx_count)]

    state = jax.ShapeDtypeStruct((count + 16, HD), BF)
    states = pl.pallas_call(
        lambda *refs: attend_kernel(ctx_count, beams, heads, kv_count, per_kv, tokens, *refs),
        out_shape=[state] * ctx_count,
        in_specs=[SMEM] + [VMEM] * (ctx_count + 2),
        out_specs=[VMEM] * ctx_count,
        compiler_params=params(8),
        cost_estimate=cost(4 * beams * H * tokens * HD, 4 * tokens * KVH * HD),
        name="attend",
    )(lengths, *stacks, kt, vt)
    states = [states[0]] + [partner(states[k], "ctx", k) for k in range(1, ctx_count)]

    attended = pl.pallas_call(
        lambda *refs: merge_kernel(ctx_count, beams, heads, kv_count, per_kv, *refs),
        out_shape=jax.ShapeDtypeStruct((beams, heads, HD), BF),
        in_specs=[VMEM] * (1 + ctx_count),
        out_specs=VMEM,
        compiler_params=params(8),
        name="merge",
    )(stack, *states)
    rows_of = [attended] + [partner(attended, "beam", k) for k in range(1, beams)]

    columns = out_weight.shape[1] // ctx_count
    parts = pl.pallas_call(
        lambda *refs: project_kernel(ctx_count, beams, heads, *refs),
        out_shape=[jax.ShapeDtypeStruct((beams, columns), F32)] * ctx_count,
        in_specs=[SMEM] + [VMEM] * (beams + 1),
        out_specs=[VMEM] * ctx_count,
        scratch_shapes=[pltpu.VMEM((8 * heads, HD), F32), pltpu.VMEM((8, heads * HD), BF)],
        compiler_params=params(8),
        cost_estimate=cost(16 * out_weight.size, 2 * out_weight.size),
        name="project",
    )(parents, *rows_of, out_weight)
    total = parts[0]
    for k in range(1, ctx_count):
        total = total + partner(parts[k], "ctx", k)
    return total.astype(BF)


def solution(mesh):
    placed = (
        P(("groups", "beam"), "ctx"),
        P(("groups", "beam"), None),
        P(("groups", "beam"), None),
        P(("groups", "beam"), "ctx", None, None),
        P(("groups", "beam"), "ctx", None, None),
        P("groups"),
        P("groups"),
        P("ctx", "beam"),
    )
    return jax.shard_map(
        per_device,
        mesh=mesh,
        in_specs=placed,
        out_specs=P("groups", ("beam", "ctx")),
        check_vma=False,
    )
```

```python
import math

import jax
import jax.numpy as jnp
from jax import lax
from jax.experimental import pallas as pl
from jax.experimental.pallas import tpu as pltpu
from jax.sharding import PartitionSpec as P


H = 128
KVH = 8
HD = 128
SPAN = 128
GROUP = H // KVH

MASKED = -1e30
SCALE = 1.0 / math.sqrt(HD)

BF = jnp.bfloat16
F32 = jnp.float32
VMEM = pl.BlockSpec(memory_space=pltpu.VMEM)
HBM = pl.BlockSpec(memory_space=pltpu.HBM)
PIECES = 4


def params(mib):
    return pltpu.CompilerParams(vmem_limit_bytes=mib << 20)


def cost(flops, moved):
    return pl.CostEstimate(flops=flops, bytes_accessed=moved, transcendentals=0)


def partners(arrays, axis):
    length = lax.axis_size(axis)
    found = []
    for k in range(1, length):
        array = arrays[k] if isinstance(arrays, (list, tuple)) else arrays
        found.append(lax.ppermute(array, axis, [(i, i ^ k) for i in range(length)]))
    return found


def pack_kernel(heads, kv_count, q_hbm, k_hbm, v_hbm, out_ref, q_ref, k_ref, v_ref, rows, sems):
    copies = [
        pltpu.make_async_copy(src, dst, sems.at[n])
        for n, (src, dst) in enumerate(((q_hbm, q_ref), (k_hbm, k_ref), (v_hbm, v_ref)))
    ]
    for copy in copies:
        copy.start()
    start = lax.axis_index("ctx") * heads // GROUP
    rows[...] = jnp.zeros_like(rows)
    for copy in copies:
        copy.wait()
    for h in range(heads):
        rows[h : h + 1, :] = q_ref[:, h * HD : (h + 1) * HD].astype(F32)
    for r in range(kv_count):
        here = pl.ds(pl.multiple_of((start + r) * HD, HD), HD)
        rows[heads + r : heads + r + 1, :] = k_ref[:, here].astype(F32)
        rows[heads + kv_count + r : heads + kv_count + r + 1, :] = v_ref[:, here].astype(F32)
    out_ref[...] = rows[...].astype(BF)


def fetch_kernel(piece, w_hbm, out_ref, sem):
    rows = out_ref.shape[0]
    copy = pltpu.make_async_copy(w_hbm.at[pl.ds(piece * rows, rows)], out_ref, sem)
    copy.start()
    copy.wait()


def split3(x):
    a = x.astype(BF)
    rest = x - a.astype(F32)
    b = rest.astype(BF)
    c = (rest - b.astype(F32)).astype(BF)
    return a, b, c


def eye(rows):
    shape = (rows, HD)
    return lax.broadcasted_iota(jnp.int32, shape, 0) == lax.broadcasted_iota(jnp.int32, shape, 1)


def attend_kernel(ctx_count, beams, heads, kv_count, per_kv, tokens, *refs):
    lengths_hbm, parents_hbm, w_hbm, kt, vt = refs[:5]
    stacks, outs = refs[5 : 5 + ctx_count], refs[5 + ctx_count : 5 + 2 * ctx_count]
    piece, lengths, parents, sems = refs[5 + 2 * ctx_count :]
    small = [
        pltpu.make_async_copy(lengths_hbm, lengths, sems.at[0]),
        pltpu.make_async_copy(parents_hbm, parents, sems.at[1]),
    ]
    large = pltpu.make_async_copy(w_hbm.at[pl.ds(piece.shape[0], piece.shape[0])], piece, sems.at[2])
    for copy in small:
        copy.start()
    large.start()
    b = lax.axis_index("beam")
    c = lax.axis_index("ctx")
    for copy in small:
        copy.wait()
    limit = lengths[b] * SPAN - c * tokens
    rows = beams * per_kv
    keep = lax.broadcasted_iota(jnp.int32, (rows, tokens), 1) < limit
    for k in range(ctx_count):
        first = (c ^ k) * heads // GROUP
        lses = []
        for r in range(kv_count):
            q = stacks[k][:, r * per_kv : (r + 1) * per_kv, :].astype(F32)
            q = q.reshape(rows, HD).astype(BF)
            s = lax.dot_general(q, kt[first + r], (((1,), (1,)), ((), ())), preferred_element_type=F32)
            s = jnp.where(keep, s * SCALE, MASKED)
            peak = jnp.max(s, axis=-1, keepdims=True)
            w = jnp.where(keep, jnp.exp(s - peak), 0.0)
            total = jnp.sum(w, axis=-1, keepdims=True)
            o = jnp.dot(w.astype(BF), vt[first + r], preferred_element_type=F32)
            some = total > 0.0
            safe = jnp.where(some, total, 1.0)
            outs[k][r * rows : (r + 1) * rows, :] = (o / safe).astype(BF)
            lses.append(jnp.where(some, peak + jnp.log(safe), MASKED))
        lse = jnp.concatenate(lses, axis=0) if kv_count > 1 else lses[0]
        count = kv_count * rows
        line = jnp.sum(jnp.where(eye(count), lse, 0.0), axis=0, keepdims=True)
        parts = [p.astype(F32) for p in split3(line)]
        which = lax.broadcasted_iota(jnp.int32, (16, HD), 0)
        stats = jnp.where(which == 0, parts[0], jnp.where(which == 1, parts[1], jnp.where(which == 2, parts[2], 0.0)))
        if k == 0:
            child = lax.broadcasted_iota(jnp.int32, (16, HD), 1) % rows // per_kv
            for i in range(beams):
                stats = jnp.where((which == 3) & (child == i) & (parents[b ^ i] == b), 1.0, stats)
        outs[k][count : count + 16, :] = stats.astype(BF)
    large.wait()


def merge_kernel(ctx_count, beams, heads, kv_count, per_kv, *refs):
    stack, states, out_ref = refs[0], refs[1 : 1 + ctx_count], refs[1 + ctx_count]
    b = lax.axis_index("beam")
    rows = beams * per_kv
    count = kv_count * rows
    diagonal = eye(count)
    own, value = [], []
    for r in range(kv_count):
        q = stack[:, r * per_kv : (r + 1) * per_kv, :].astype(F32)
        key = stack[:, heads + r : heads + r + 1, :].astype(F32)
        own.append(jnp.sum(q * key, axis=-1, keepdims=True).reshape(rows, 1) * SCALE)
        v = stack[:, heads + kv_count + r : heads + kv_count + r + 1, :].astype(F32)
        value.append(jnp.broadcast_to(v, (beams, per_kv, HD)).reshape(rows, HD))
    own = jnp.concatenate(own, axis=0) if kv_count > 1 else own[0]
    value = jnp.concatenate(value, axis=0) if kv_count > 1 else value[0]
    lses = []
    for k in range(ctx_count):
        line = states[k][count : count + 16, :].astype(F32)
        if k == 0:
            mine = jnp.sum(jnp.where(diagonal, line[3:4], 0.0), axis=-1, keepdims=True)
        line = line[0:1] + line[1:2] + line[2:3]
        lses.append(jnp.sum(jnp.where(diagonal, line, 0.0), axis=-1, keepdims=True))
    peak = own
    for lse in lses:
        peak = jnp.maximum(peak, lse)
    weight = jnp.exp(own - peak)
    total = weight
    blended = weight * value
    for k in range(ctx_count):
        weight = jnp.exp(lses[k] - peak)
        total = total + weight
        blended = blended + weight * states[k][0:count, :].astype(F32)
    result = jnp.where(mine > 0.0, blended / total, 0.0).astype(BF)
    for r in range(kv_count):
        for i in range(beams):
            at = r * rows + i * per_kv
            out_ref[b ^ i, r * per_kv : (r + 1) * per_kv, :] = result[at : at + per_kv, :]


def project_kernel(ctx_count, beams, heads, *refs):
    rows_of, pieces, w_hbm = refs[:beams], refs[beams : beams + PIECES - 1], refs[beams + PIECES - 1]
    outs = refs[beams + PIECES : beams + PIECES + ctx_count]
    last, laid, wide, sem = refs[beams + PIECES + ctx_count :]
    depth = last.shape[0]
    copy = pltpu.make_async_copy(w_hbm.at[pl.ds((PIECES - 1) * depth, depth)], last, sem)
    copy.start()
    c = lax.axis_index("ctx")
    laid[...] = jnp.zeros_like(laid)
    for i in range(beams):
        row = rows_of[0][i].astype(F32)
        for k in range(1, beams):
            row = row + rows_of[k][i].astype(F32)
        laid[i * heads : (i + 1) * heads, :] = row
    for h in range(heads):
        wide[:, h * HD : (h + 1) * HD] = laid[pl.ds(h, 8, stride=heads), :].astype(BF)
    columns = last.shape[1] // ctx_count
    step = min(512, columns)

    def share(k, j, n, ref):
        at = pl.multiple_of((c ^ k) * columns + j * step, 128)
        return jnp.dot(
            wide[:, n * depth : (n + 1) * depth], ref[:, pl.ds(at, step)], preferred_element_type=F32
        )[:beams]

    for k in range(ctx_count):
        for j in range(columns // step):
            outs[k][:, j * step : (j + 1) * step] = sum(share(k, j, n, ref) for n, ref in enumerate(pieces))
    copy.wait()
    for k in range(ctx_count):
        for j in range(columns // step):
            outs[k][:, j * step : (j + 1) * step] += share(k, j, PIECES - 1, last)


def step(queries, new_keys, new_values, cache_keys, cache_values, parents, lengths, out_weight):
    ctx_count = lax.axis_size("ctx")
    beams = lax.axis_size("beam")
    heads = queries.shape[1] // HD
    tokens = cache_keys.shape[1]
    kv_count = max(1, heads // GROUP)
    per_kv = min(heads, GROUP)
    packet_rows = -(-(heads + 2 * kv_count) // 16) * 16
    count = beams * heads

    queries, new_keys, new_values, parents, lengths, out_weight = (
        pltpu.with_memory_space_constraint(x, pltpu.HBM)
        for x in (queries, new_keys, new_values, parents, lengths, out_weight)
    )
    depth = out_weight.shape[0] // PIECES
    piece = jax.ShapeDtypeStruct((depth, out_weight.shape[1]), BF)

    def fetch(n):
        return pl.pallas_call(
            lambda *refs: fetch_kernel(n, *refs),
            out_shape=piece,
            in_specs=[HBM],
            out_specs=VMEM,
            scratch_shapes=[pltpu.SemaphoreType.DMA],
            compiler_params=params(4),
            cost_estimate=cost(0, 2 * piece.size),
        )(out_weight)

    packet = pl.pallas_call(
        lambda *refs: pack_kernel(heads, kv_count, *refs),
        out_shape=jax.ShapeDtypeStruct((packet_rows, HD), BF),
        in_specs=[HBM] * 3,
        out_specs=VMEM,
        scratch_shapes=[pltpu.VMEM(x.shape, BF) for x in (queries, new_keys, new_values)]
        + [pltpu.VMEM((packet_rows, HD), F32), pltpu.SemaphoreType.DMA((3,))],
        compiler_params=params(4),
        name="pack",
    )(queries, new_keys, new_values)
    kt = jnp.transpose(cache_keys[0], (1, 0, 2))
    vt = jnp.transpose(cache_values[0], (1, 0, 2))
    stack = jnp.stack([packet] + partners(packet, "beam"))
    stacks = [stack] + partners(stack, "ctx")
    first_piece = fetch(0)

    state = jax.ShapeDtypeStruct((count + 16, HD), BF)
    *states, second_piece = pl.pallas_call(
        lambda *refs: attend_kernel(ctx_count, beams, heads, kv_count, per_kv, tokens, *refs),
        out_shape=[state] * ctx_count + [piece],
        in_specs=[HBM] * 3 + [VMEM] * (ctx_count + 2),
        out_specs=[VMEM] * (ctx_count + 1),
        scratch_shapes=[pltpu.SMEM(lengths.shape, jnp.int32)] * 2 + [pltpu.SemaphoreType.DMA((3,))],
        compiler_params=params(8),
        cost_estimate=cost(4 * beams * H * tokens * HD, 2 * piece.size),
        name="attend",
    )(lengths, parents, out_weight, kt, vt, *stacks)
    states = [states[0]] + partners(states, "ctx")
    third_piece = fetch(2)

    attended = pl.pallas_call(
        lambda *refs: merge_kernel(ctx_count, beams, heads, kv_count, per_kv, *refs),
        out_shape=jax.ShapeDtypeStruct((beams, heads, HD), BF),
        in_specs=[VMEM] * (1 + ctx_count),
        out_specs=VMEM,
        compiler_params=params(8),
        name="merge",
    )(stack, *states)
    rows_of = [attended] + partners(attended, "beam")

    columns = out_weight.shape[1] // ctx_count
    parts = pl.pallas_call(
        lambda *refs: project_kernel(ctx_count, beams, heads, *refs),
        out_shape=[jax.ShapeDtypeStruct((beams, columns), F32)] * ctx_count,
        in_specs=[VMEM] * (beams + PIECES - 1) + [HBM],
        out_specs=[VMEM] * ctx_count,
        scratch_shapes=[
            pltpu.VMEM(piece.shape, BF),
            pltpu.VMEM((8 * heads, HD), F32),
            pltpu.VMEM((8, heads * HD), BF),
            pltpu.SemaphoreType.DMA,
        ],
        compiler_params=params(16),
        cost_estimate=cost(16 * out_weight.size, 2 * piece.size),
        name="project",
    )(*rows_of, first_piece, second_piece, third_piece, out_weight)
    total = parts[0]
    for part in partners(parts, "ctx"):
        total = total + part
    return total.astype(BF)


def solution(mesh):
    placed = (
        P(("groups", "beam"), "ctx"),
        P(("groups", "beam"), None),
        P(("groups", "beam"), None),
        P(("groups", "beam"), "ctx", None, None),
        P(("groups", "beam"), "ctx", None, None),
        P("groups"),
        P("groups"),
        P("ctx", "beam"),
    )
    return jax.shard_map(
        step,
        mesh=mesh,
        in_specs=placed,
        out_specs=P("groups", ("beam", "ctx")),
        check_vma=False,
    )
```

```python
import math

import jax
import jax.numpy as jnp
from jax import lax
from jax.experimental import pallas as pl
from jax.experimental.pallas import tpu as pltpu
from jax.sharding import PartitionSpec as P


H = 128
KVH = 8
HD = 128
SPAN = 128
GROUP = H // KVH

MASKED = -1e30
SCALE = 1.0 / math.sqrt(HD)

BF = jnp.bfloat16
F32 = jnp.float32
VMEM = pl.BlockSpec(memory_space=pltpu.VMEM)
HBM = pl.BlockSpec(memory_space=pltpu.HBM)
SHARES = (4, 8, 4, 10, 6)


def params(mib):
    return pltpu.CompilerParams(vmem_limit_bytes=mib << 20)


def cost(flops, moved):
    return pl.CostEstimate(flops=flops, bytes_accessed=moved, transcendentals=0)


def partners(arrays, axis):
    length = lax.axis_size(axis)
    found = []
    for k in range(1, length):
        array = arrays[k] if isinstance(arrays, (list, tuple)) else arrays
        found.append(lax.ppermute(array, axis, [(i, i ^ k) for i in range(length)]))
    return found


def pack_kernel(heads, kv_count, q_hbm, k_hbm, v_hbm, out_ref, q_ref, k_ref, v_ref, rows, sems):
    copies = [
        pltpu.make_async_copy(src, dst, sems.at[n])
        for n, (src, dst) in enumerate(((q_hbm, q_ref), (k_hbm, k_ref), (v_hbm, v_ref)))
    ]
    for copy in copies:
        copy.start()
    start = lax.axis_index("ctx") * heads // GROUP
    rows[...] = jnp.zeros_like(rows)
    for copy in copies:
        copy.wait()
    for h in range(heads):
        rows[h : h + 1, :] = q_ref[:, h * HD : (h + 1) * HD].astype(F32)
    for r in range(kv_count):
        here = pl.ds(pl.multiple_of((start + r) * HD, HD), HD)
        rows[heads + r : heads + r + 1, :] = k_ref[:, here].astype(F32)
        rows[heads + kv_count + r : heads + kv_count + r + 1, :] = v_ref[:, here].astype(F32)
    out_ref[...] = rows[...].astype(BF)


def fetch_kernel(start, w_hbm, out_ref, sem):
    copy = pltpu.make_async_copy(w_hbm.at[pl.ds(start, out_ref.shape[0])], out_ref, sem)
    copy.start()
    copy.wait()


def split3(x):
    a = x.astype(BF)
    rest = x - a.astype(F32)
    b = rest.astype(BF)
    c = (rest - b.astype(F32)).astype(BF)
    return a, b, c


def eye(rows):
    shape = (rows, HD)
    return lax.broadcasted_iota(jnp.int32, shape, 0) == lax.broadcasted_iota(jnp.int32, shape, 1)


def attend_kernel(slots, start, beams, heads, kv_count, per_kv, tokens, *refs):
    n = len(slots)
    lengths_hbm, parents_hbm, w_hbm, kt, vt = refs[:5]
    stacks, outs = refs[5 : 5 + n], refs[5 + n : 5 + 2 * n]
    piece, lengths, parents, sems = refs[5 + 2 * n :]
    small = [
        pltpu.make_async_copy(lengths_hbm, lengths, sems.at[0]),
        pltpu.make_async_copy(parents_hbm, parents, sems.at[1]),
    ]
    large = pltpu.make_async_copy(w_hbm.at[pl.ds(start, piece.shape[0])], piece, sems.at[2])
    for copy in small:
        copy.start()
    large.start()
    b = lax.axis_index("beam")
    c = lax.axis_index("ctx")
    rows = beams * per_kv
    count = kv_count * rows
    pairs = [(i, r) for i in range(n) for r in range(kv_count)]

    def kv_head(i, r):
        return (c ^ slots[i]) * heads // GROUP + r

    scores = []
    for i, r in pairs:
        q = stacks[i][:, r * per_kv : (r + 1) * per_kv, :].astype(F32)
        q = q.reshape(rows, HD).astype(BF)
        scores.append(
            lax.dot_general(q, kt[kv_head(i, r)], (((1,), (1,)), ((), ())), preferred_element_type=F32)
        )
    for copy in small:
        copy.wait()
    limit = lengths[b] * SPAN - c * tokens
    keep = lax.broadcasted_iota(jnp.int32, (rows, tokens), 1) < limit
    scores = [jnp.where(keep, s * SCALE, MASKED) for s in scores]
    peaks = [jnp.max(s, axis=-1, keepdims=True) for s in scores]
    weights = [jnp.where(keep, jnp.exp(s - m), 0.0) for s, m in zip(scores, peaks)]
    totals = [jnp.sum(w, axis=-1, keepdims=True) for w in weights]
    blended = [
        jnp.dot(w.astype(BF), vt[kv_head(i, r)], preferred_element_type=F32)
        for w, (i, r) in zip(weights, pairs)
    ]
    safe = [jnp.where(t > 0.0, t, 1.0) for t in totals]
    lses = [jnp.where(t > 0.0, m + jnp.log(f), MASKED) for t, m, f in zip(totals, peaks, safe)]
    which = lax.broadcasted_iota(jnp.int32, (16, HD), 0)
    diagonal = eye(count)
    for i in range(n):
        mine = slice(i * kv_count, (i + 1) * kv_count)
        outs[i][0:count, :] = jnp.concatenate(
            [(o / f).astype(BF) for o, f in zip(blended[mine], safe[mine])], axis=0
        )
        lse = jnp.concatenate(lses[mine], axis=0)
        line = jnp.sum(jnp.where(diagonal, lse, 0.0), axis=0, keepdims=True)
        parts = [p.astype(F32) for p in split3(line)]
        stats = jnp.where(which == 0, parts[0], jnp.where(which == 1, parts[1], jnp.where(which == 2, parts[2], 0.0)))
        if slots[i] == 0:
            child = lax.broadcasted_iota(jnp.int32, (16, HD), 1) % rows // per_kv
            for k in range(beams):
                stats = jnp.where((which == 3) & (child == k) & (parents[b ^ k] == b), 1.0, stats)
        outs[i][count : count + 16, :] = stats.astype(BF)
    large.wait()


def merge_kernel(ctx_count, beams, heads, kv_count, per_kv, *refs):
    stack, states, out_ref = refs[0], refs[1 : 1 + ctx_count], refs[1 + ctx_count]
    b = lax.axis_index("beam")
    rows = beams * per_kv
    count = kv_count * rows
    diagonal = eye(count)
    own, value = [], []
    for r in range(kv_count):
        q = stack[:, r * per_kv : (r + 1) * per_kv, :].astype(F32)
        key = stack[:, heads + r : heads + r + 1, :].astype(F32)
        own.append(jnp.sum(q * key, axis=-1, keepdims=True).reshape(rows, 1) * SCALE)
        v = stack[:, heads + kv_count + r : heads + kv_count + r + 1, :].astype(F32)
        value.append(jnp.broadcast_to(v, (beams, per_kv, HD)).reshape(rows, HD))
    own = jnp.concatenate(own, axis=0) if kv_count > 1 else own[0]
    value = jnp.concatenate(value, axis=0) if kv_count > 1 else value[0]
    lses = []
    for k in range(ctx_count):
        line = states[k][count : count + 16, :].astype(F32)
        if k == 0:
            mine = jnp.sum(jnp.where(diagonal, line[3:4], 0.0), axis=-1, keepdims=True)
        line = line[0:1] + line[1:2] + line[2:3]
        lses.append(jnp.sum(jnp.where(diagonal, line, 0.0), axis=-1, keepdims=True))
    peak = own
    for lse in lses:
        peak = jnp.maximum(peak, lse)
    weight = jnp.exp(own - peak)
    total = weight
    blended = weight * value
    for k in range(ctx_count):
        weight = jnp.exp(lses[k] - peak)
        total = total + weight
        blended = blended + weight * states[k][0:count, :].astype(F32)
    result = jnp.where(mine > 0.0, blended / total, 0.0).astype(BF)
    for r in range(kv_count):
        for i in range(beams):
            at = r * rows + i * per_kv
            out_ref[b ^ i, r * per_kv : (r + 1) * per_kv, :] = result[at : at + per_kv, :]


def chunk(rows, pieces, bounds, beams, at, width):
    return sum(
        jnp.dot(rows[:, lo:hi], ref[:, pl.ds(at, width)], preferred_element_type=F32)
        for ref, lo, hi in zip(pieces, bounds, bounds[1:])
    )[:beams]


def project_kernel(ctx_count, beams, heads, bounds, *refs):
    rows_of, pieces, w_hbm = refs[:beams], refs[beams : beams + 4], refs[beams + 4]
    outs, (last, wide), (laid, sem) = refs[beams + 5 : -4], refs[-4:-2], refs[-2:]
    copy = pltpu.make_async_copy(w_hbm.at[pl.ds(bounds[4], last.shape[0])], last, sem)
    copy.start()
    c = lax.axis_index("ctx")
    laid[...] = jnp.zeros_like(laid)
    for i in range(beams):
        row = rows_of[0][i].astype(F32)
        for k in range(1, beams):
            row = row + rows_of[k][i].astype(F32)
        laid[i * heads : (i + 1) * heads, :] = row
    for h in range(heads):
        wide[:, h * HD : (h + 1) * HD] = laid[pl.ds(h, 8, stride=heads), :].astype(BF)
    columns = last.shape[1] // ctx_count
    width = min(512, columns)
    places = [(k, j) for k in range(1, ctx_count) for j in range(0, columns, width)]
    for k, j in places:
        at = pl.multiple_of((c ^ k) * columns + j, 128)
        outs[k - 1][:, j : j + width] = chunk(wide, pieces, bounds[:5], beams, at, width)
    copy.wait()
    for k, j in places:
        at = pl.multiple_of((c ^ k) * columns + j, 128)
        outs[k - 1][:, j : j + width] += chunk(wide, [last], bounds[4:], beams, at, width)


def home_kernel(ctx_count, beams, bounds, wide, *refs):
    pieces, out_ref = refs[:-1], refs[-1]
    columns = pieces[0].shape[1] // ctx_count
    width = min(512, columns)
    for j in range(0, columns, width):
        at = pl.multiple_of(lax.axis_index("ctx") * columns + j, 128)
        out_ref[:, j : j + width] = chunk(wide, pieces, bounds, beams, at, width)


def step(queries, new_keys, new_values, cache_keys, cache_values, parents, lengths, out_weight):
    ctx_count = lax.axis_size("ctx")
    beams = lax.axis_size("beam")
    heads = queries.shape[1] // HD
    tokens = cache_keys.shape[1]
    kv_count = max(1, heads // GROUP)
    per_kv = min(heads, GROUP)
    packet_rows = -(-(heads + 2 * kv_count) // 16) * 16
    count = beams * heads

    queries, new_keys, new_values, parents, lengths, out_weight = (
        pltpu.with_memory_space_constraint(x, pltpu.HBM)
        for x in (queries, new_keys, new_values, parents, lengths, out_weight)
    )
    bounds = [heads * sum(SHARES[:n]) // sum(SHARES) * HD for n in range(len(SHARES) + 1)]
    piece = [jax.ShapeDtypeStruct((hi - lo, out_weight.shape[1]), BF) for lo, hi in zip(bounds, bounds[1:])]

    def fetch(n):
        return pl.pallas_call(
            lambda *refs: fetch_kernel(bounds[n], *refs),
            out_shape=piece[n],
            in_specs=[HBM],
            out_specs=VMEM,
            scratch_shapes=[pltpu.SemaphoreType.DMA],
            compiler_params=params(4),
            cost_estimate=cost(0, 2 * piece[n].size),
        )(out_weight)

    def attend(slots, n):
        return pl.pallas_call(
            lambda *refs: attend_kernel(slots, bounds[n], beams, heads, kv_count, per_kv, tokens, *refs),
            out_shape=[jax.ShapeDtypeStruct((count + 16, HD), BF)] * len(slots) + [piece[n]],
            in_specs=[HBM] * 3 + [VMEM] * (len(slots) + 2),
            out_specs=[VMEM] * (len(slots) + 1),
            scratch_shapes=[pltpu.SMEM(lengths.shape, jnp.int32)] * 2 + [pltpu.SemaphoreType.DMA((3,))],
            compiler_params=params(12),
            cost_estimate=cost(4 * count * len(slots) * tokens * HD, 2 * piece[n].size),
        )(lengths, parents, out_weight, kt, vt, *[stacks[k] for k in slots])

    packet = pl.pallas_call(
        lambda *refs: pack_kernel(heads, kv_count, *refs),
        out_shape=jax.ShapeDtypeStruct((packet_rows, HD), BF),
        in_specs=[HBM] * 3,
        out_specs=VMEM,
        scratch_shapes=[pltpu.VMEM(x.shape, BF) for x in (queries, new_keys, new_values)]
        + [pltpu.VMEM((packet_rows, HD), F32), pltpu.SemaphoreType.DMA((3,))],
        compiler_params=params(4),
        name="pack",
    )(queries, new_keys, new_values)
    kt = jnp.transpose(cache_keys[0], (1, 0, 2))
    vt = jnp.transpose(cache_values[0], (1, 0, 2))
    stack = jnp.stack([packet] + partners(packet, "beam"))
    stacks = [stack] + partners(stack, "ctx")
    own_state, piece0 = attend((0,), 0)
    *states, piece1 = attend(tuple(range(1, ctx_count)), 1)
    states = [own_state] + partners([None] + states, "ctx")
    piece2 = fetch(2)

    attended = pl.pallas_call(
        lambda *refs: merge_kernel(ctx_count, beams, heads, kv_count, per_kv, *refs),
        out_shape=jax.ShapeDtypeStruct((beams, heads, HD), BF),
        in_specs=[VMEM] * (1 + ctx_count),
        out_specs=VMEM,
        compiler_params=params(8),
        name="merge",
    )(stack, *states)
    rows_of = [attended] + partners(attended, "beam")

    piece3 = fetch(3)

    columns = out_weight.shape[1] // ctx_count
    part = jax.ShapeDtypeStruct((beams, columns), F32)
    wide = jax.ShapeDtypeStruct((8, heads * HD), BF)
    *parts, piece4, wide = pl.pallas_call(
        lambda *refs: project_kernel(ctx_count, beams, heads, bounds, *refs),
        out_shape=[part] * (ctx_count - 1) + [piece[4], wide],
        in_specs=[VMEM] * (beams + 4) + [HBM],
        out_specs=[VMEM] * (ctx_count + 1),
        scratch_shapes=[pltpu.VMEM((8 * heads, HD), F32), pltpu.SemaphoreType.DMA],
        compiler_params=params(8),
        cost_estimate=cost(12 * out_weight.size, 2 * piece[4].size),
        name="project",
    )(*rows_of, piece0, piece1, piece2, piece3, out_weight)
    others = partners([None] + parts, "ctx")
    total = pl.pallas_call(
        lambda *refs: home_kernel(ctx_count, beams, bounds, *refs),
        out_shape=part,
        in_specs=[VMEM] * 6,
        out_specs=VMEM,
        compiler_params=params(4),
        cost_estimate=cost(4 * out_weight.size, 0),
        name="home",
    )(wide, piece0, piece1, piece2, piece3, piece4)
    for other in others:
        total = total + other
    return total.astype(BF)


def solution(mesh):
    placed = (
        P(("groups", "beam"), "ctx"),
        P(("groups", "beam"), None),
        P(("groups", "beam"), None),
        P(("groups", "beam"), "ctx", None, None),
        P(("groups", "beam"), "ctx", None, None),
        P("groups"),
        P("groups"),
        P("ctx", "beam"),
    )
    return jax.shard_map(
        step,
        mesh=mesh,
        in_specs=placed,
        out_specs=P("groups", ("beam", "ctx")),
        check_vma=False,
    )
```

```python
import math

import jax
import jax.numpy as jnp
from jax import lax
from jax.experimental import pallas as pl
from jax.experimental.pallas import tpu as pltpu
from jax.sharding import PartitionSpec as P


H = 128
KVH = 8
HD = 128
SPAN = 128
GROUP = H // KVH

MASKED = -1e30
SCALE = 1.0 / math.sqrt(HD)

BF = jnp.bfloat16
F32 = jnp.float32
VMEM = pl.BlockSpec(memory_space=pltpu.VMEM)
HBM = pl.BlockSpec(memory_space=pltpu.HBM)
SHARES = (5, 5, 5, 10, 7)


def params(mib):
    return pltpu.CompilerParams(vmem_limit_bytes=mib << 20)


def cost(flops, moved):
    return pl.CostEstimate(flops=flops, bytes_accessed=moved, transcendentals=0)


def partner(array, axis, k):
    return lax.ppermute(array, axis, [(i, i ^ k) for i in range(lax.axis_size(axis))])


def partners(arrays, axis):
    each = isinstance(arrays, (list, tuple))
    return [partner(arrays[k] if each else arrays, axis, k) for k in range(1, lax.axis_size(axis))]


def pack_kernel(heads, kv_count, q_hbm, k_hbm, v_hbm, out_ref, q_ref, k_ref, v_ref, rows, sems):
    copies = [
        pltpu.make_async_copy(src, dst, sems.at[n])
        for n, (src, dst) in enumerate(((q_hbm, q_ref), (k_hbm, k_ref), (v_hbm, v_ref)))
    ]
    for copy in copies:
        copy.start()
    start = lax.axis_index("ctx") * heads // GROUP
    rows[...] = jnp.zeros_like(rows)
    for copy in copies:
        copy.wait()
    for h in range(heads):
        rows[h : h + 1, :] = q_ref[:, h * HD : (h + 1) * HD].astype(F32)
    for r in range(kv_count):
        here = pl.ds(pl.multiple_of((start + r) * HD, HD), HD)
        rows[heads + r : heads + r + 1, :] = k_ref[:, here].astype(F32)
        rows[heads + kv_count + r : heads + kv_count + r + 1, :] = v_ref[:, here].astype(F32)
    out_ref[...] = rows[...].astype(BF)


def fetch_kernel(start, w_hbm, out_ref, sem):
    copy = pltpu.make_async_copy(w_hbm.at[pl.ds(start, out_ref.shape[0])], out_ref, sem)
    copy.start()
    copy.wait()


def split3(x):
    a = x.astype(BF)
    rest = x - a.astype(F32)
    b = rest.astype(BF)
    c = (rest - b.astype(F32)).astype(BF)
    return a, b, c


def eye(rows):
    shape = (rows, HD)
    return lax.broadcasted_iota(jnp.int32, shape, 0) == lax.broadcasted_iota(jnp.int32, shape, 1)


def attend_kernel(slots, start, beams, heads, kv_count, per_kv, tokens, *refs):
    n = len(slots)
    lengths_hbm, parents_hbm, w_hbm, kt, vt = refs[:5]
    stacks, outs = refs[5 : 5 + n], refs[5 + n : 5 + 2 * n]
    piece, lengths, parents, sems = refs[5 + 2 * n :]
    small = [
        pltpu.make_async_copy(lengths_hbm, lengths, sems.at[0]),
        pltpu.make_async_copy(parents_hbm, parents, sems.at[1]),
    ]
    large = pltpu.make_async_copy(w_hbm.at[pl.ds(start, piece.shape[0])], piece, sems.at[2])
    for copy in small:
        copy.start()
    large.start()
    b = lax.axis_index("beam")
    c = lax.axis_index("ctx")
    rows = beams * per_kv
    count = kv_count * rows
    pairs = [(i, r) for i in range(n) for r in range(kv_count)]

    def kv_head(i, r):
        return (c ^ slots[i]) * heads // GROUP + r

    scores = []
    for i, r in pairs:
        q = stacks[i][:, r * per_kv : (r + 1) * per_kv, :].astype(F32)
        q = q.reshape(rows, HD).astype(BF)
        scores.append(
            lax.dot_general(q, kt[kv_head(i, r)], (((1,), (1,)), ((), ())), preferred_element_type=F32)
        )
    for copy in small:
        copy.wait()
    limit = lengths[b] * SPAN - c * tokens
    keep = lax.broadcasted_iota(jnp.int32, (rows, tokens), 1) < limit
    scores = [jnp.where(keep, s * SCALE, MASKED) for s in scores]
    peaks = [jnp.max(s, axis=-1, keepdims=True) for s in scores]
    weights = [jnp.where(keep, jnp.exp(s - m), 0.0) for s, m in zip(scores, peaks)]
    totals = [jnp.sum(w, axis=-1, keepdims=True) for w in weights]
    blended = [
        jnp.dot(w.astype(BF), vt[kv_head(i, r)], preferred_element_type=F32)
        for w, (i, r) in zip(weights, pairs)
    ]
    safe = [jnp.where(t > 0.0, t, 1.0) for t in totals]
    lses = [jnp.where(t > 0.0, m + jnp.log(f), MASKED) for t, m, f in zip(totals, peaks, safe)]
    which = lax.broadcasted_iota(jnp.int32, (16, HD), 0)
    diagonal = eye(count)
    for i in range(n):
        mine = slice(i * kv_count, (i + 1) * kv_count)
        outs[i][0:count, :] = jnp.concatenate(
            [(o / f).astype(BF) for o, f in zip(blended[mine], safe[mine])], axis=0
        )
        lse = jnp.concatenate(lses[mine], axis=0)
        line = jnp.sum(jnp.where(diagonal, lse, 0.0), axis=0, keepdims=True)
        parts = [p.astype(F32) for p in split3(line)]
        stats = jnp.where(which == 0, parts[0], jnp.where(which == 1, parts[1], jnp.where(which == 2, parts[2], 0.0)))
        if slots[i] == 0:
            child = lax.broadcasted_iota(jnp.int32, (16, HD), 1) % rows // per_kv
            for k in range(beams):
                stats = jnp.where((which == 3) & (child == k) & (parents[b ^ k] == b), 1.0, stats)
        outs[i][count : count + 16, :] = stats.astype(BF)
    large.wait()


def merge_kernel(ctx_count, beams, heads, kv_count, per_kv, *refs):
    stack, states, out_ref = refs[0], refs[1 : 1 + ctx_count], refs[1 + ctx_count]
    b = lax.axis_index("beam")
    rows = beams * per_kv
    count = kv_count * rows
    diagonal = eye(count)
    own, value = [], []
    for r in range(kv_count):
        q = stack[:, r * per_kv : (r + 1) * per_kv, :].astype(F32)
        key = stack[:, heads + r : heads + r + 1, :].astype(F32)
        own.append(jnp.sum(q * key, axis=-1, keepdims=True).reshape(rows, 1) * SCALE)
        v = stack[:, heads + kv_count + r : heads + kv_count + r + 1, :].astype(F32)
        value.append(jnp.broadcast_to(v, (beams, per_kv, HD)).reshape(rows, HD))
    own = jnp.concatenate(own, axis=0) if kv_count > 1 else own[0]
    value = jnp.concatenate(value, axis=0) if kv_count > 1 else value[0]
    lses = []
    for k in range(ctx_count):
        line = states[k][count : count + 16, :].astype(F32)
        if k == 0:
            mine = jnp.sum(jnp.where(diagonal, line[3:4], 0.0), axis=-1, keepdims=True)
        line = line[0:1] + line[1:2] + line[2:3]
        lses.append(jnp.sum(jnp.where(diagonal, line, 0.0), axis=-1, keepdims=True))
    peak = own
    for lse in lses:
        peak = jnp.maximum(peak, lse)
    weight = jnp.exp(own - peak)
    total = weight
    blended = weight * value
    for k in range(ctx_count):
        weight = jnp.exp(lses[k] - peak)
        total = total + weight
        blended = blended + weight * states[k][0:count, :].astype(F32)
    result = jnp.where(mine > 0.0, blended / total, 0.0).astype(BF)
    for r in range(kv_count):
        for i in range(beams):
            at = r * rows + i * per_kv
            out_ref[b ^ i, r * per_kv : (r + 1) * per_kv, :] = result[at : at + per_kv, :]


def chunk(rows, pieces, bounds, beams, at, width):
    return sum(
        jnp.dot(rows[:, lo:hi], ref[:, pl.ds(at, width)], preferred_element_type=F32)
        for ref, lo, hi in zip(pieces, bounds, bounds[1:])
    )[:beams]


def project_kernel(ctx_count, far, beams, heads, bounds, *refs):
    rows_of, pieces, w_hbm = refs[:beams], refs[beams : beams + 4], refs[beams + 4]
    outs, (last, wide), (laid, sem) = refs[beams + 5 : -4], refs[-4:-2], refs[-2:]
    copy = pltpu.make_async_copy(w_hbm.at[pl.ds(bounds[4], last.shape[0])], last, sem)
    copy.start()
    c = lax.axis_index("ctx")
    laid[...] = jnp.zeros_like(laid)
    for i in range(beams):
        row = rows_of[0][i].astype(F32)
        for k in range(1, beams):
            row = row + rows_of[k][i].astype(F32)
        laid[i * heads : (i + 1) * heads, :] = row
    for h in range(heads):
        wide[:, h * HD : (h + 1) * HD] = laid[pl.ds(h, 8, stride=heads), :].astype(BF)
    columns = last.shape[1] // ctx_count
    width = min(512, columns)
    places = [(n, k, j) for n, k in enumerate(far) for j in range(0, columns, width)]
    for n, k, j in places:
        at = pl.multiple_of((c ^ k) * columns + j, 128)
        outs[n][:, j : j + width] = chunk(wide, pieces, bounds[:5], beams, at, width)
    copy.wait()
    for n, k, j in places:
        at = pl.multiple_of((c ^ k) * columns + j, 128)
        outs[n][:, j : j + width] += chunk(wide, [last], bounds[4:], beams, at, width)


def near_kernel(ctx_count, k, beams, bounds, wide, *refs):
    pieces, out_ref = refs[:-1], refs[-1]
    columns = pieces[0].shape[1] // ctx_count
    width = min(512, columns)
    for j in range(0, columns, width):
        at = pl.multiple_of((lax.axis_index("ctx") ^ k) * columns + j, 128)
        out_ref[:, j : j + width] = chunk(wide, pieces, bounds, beams, at, width)


def step(queries, new_keys, new_values, cache_keys, cache_values, parents, lengths, out_weight):
    ctx_count = lax.axis_size("ctx")
    beams = lax.axis_size("beam")
    heads = queries.shape[1] // HD
    tokens = cache_keys.shape[1]
    kv_count = max(1, heads // GROUP)
    per_kv = min(heads, GROUP)
    packet_rows = -(-(heads + 2 * kv_count) // 16) * 16
    count = beams * heads

    queries, new_keys, new_values, parents, lengths, out_weight = (
        pltpu.with_memory_space_constraint(x, pltpu.HBM)
        for x in (queries, new_keys, new_values, parents, lengths, out_weight)
    )
    bounds = [heads * sum(SHARES[:n]) // sum(SHARES) * HD for n in range(len(SHARES) + 1)]
    piece = [jax.ShapeDtypeStruct((hi - lo, out_weight.shape[1]), BF) for lo, hi in zip(bounds, bounds[1:])]

    def fetch(n):
        return pl.pallas_call(
            lambda *refs: fetch_kernel(bounds[n], *refs),
            out_shape=piece[n],
            in_specs=[HBM],
            out_specs=VMEM,
            scratch_shapes=[pltpu.SemaphoreType.DMA],
            compiler_params=params(4),
            cost_estimate=cost(0, 2 * piece[n].size),
        )(out_weight)

    def attend(slots, n):
        return pl.pallas_call(
            lambda *refs: attend_kernel(slots, bounds[n], beams, heads, kv_count, per_kv, tokens, *refs),
            out_shape=[jax.ShapeDtypeStruct((count + 16, HD), BF)] * len(slots) + [piece[n]],
            in_specs=[HBM] * 3 + [VMEM] * (len(slots) + 2),
            out_specs=[VMEM] * (len(slots) + 1),
            scratch_shapes=[pltpu.SMEM(lengths.shape, jnp.int32)] * 2 + [pltpu.SemaphoreType.DMA((3,))],
            compiler_params=params(12),
            cost_estimate=cost(4 * count * len(slots) * tokens * HD, 2 * piece[n].size),
        )(lengths, parents, out_weight, kt, vt, *[stacks[k] for k in slots])

    packet = pl.pallas_call(
        lambda *refs: pack_kernel(heads, kv_count, *refs),
        out_shape=jax.ShapeDtypeStruct((packet_rows, HD), BF),
        in_specs=[HBM] * 3,
        out_specs=VMEM,
        scratch_shapes=[pltpu.VMEM(x.shape, BF) for x in (queries, new_keys, new_values)]
        + [pltpu.VMEM((packet_rows, HD), F32), pltpu.SemaphoreType.DMA((3,))],
        compiler_params=params(4),
        name="pack",
    )(queries, new_keys, new_values)
    kt = jnp.transpose(cache_keys[0], (1, 0, 2))
    vt = jnp.transpose(cache_values[0], (1, 0, 2))
    stack = jnp.stack([packet] + partners(packet, "beam"))
    stacks = [stack] + partners(stack, "ctx")
    own_state, piece0 = attend((0,), 0)
    *states, piece1 = attend(tuple(range(1, ctx_count)), 1)
    states = [own_state] + partners([None] + states, "ctx")
    piece2 = fetch(2)

    attended = pl.pallas_call(
        lambda *refs: merge_kernel(ctx_count, beams, heads, kv_count, per_kv, *refs),
        out_shape=jax.ShapeDtypeStruct((beams, heads, HD), BF),
        in_specs=[VMEM] * (1 + ctx_count),
        out_specs=VMEM,
        compiler_params=params(8),
        name="merge",
    )(stack, *states)
    rows_of = [attended] + partners(attended, "beam")

    piece3 = fetch(3)

    columns = out_weight.shape[1] // ctx_count
    part = jax.ShapeDtypeStruct((beams, columns), F32)
    wide = jax.ShapeDtypeStruct((8, heads * HD), BF)
    far = tuple(range(2, ctx_count))
    *parts, piece4, wide = pl.pallas_call(
        lambda *refs: project_kernel(ctx_count, far, beams, heads, bounds, *refs),
        out_shape=[part] * len(far) + [piece[4], wide],
        in_specs=[VMEM] * (beams + 4) + [HBM],
        out_specs=[VMEM] * (len(far) + 2),
        scratch_shapes=[pltpu.VMEM((8 * heads, HD), F32), pltpu.SemaphoreType.DMA],
        compiler_params=params(8),
        cost_estimate=cost(8 * out_weight.size, 2 * piece[4].size),
        name="project",
    )(*rows_of, piece0, piece1, piece2, piece3, out_weight)

    def near(k):
        return pl.pallas_call(
            lambda *refs: near_kernel(ctx_count, k, beams, bounds, *refs),
            out_shape=part,
            in_specs=[VMEM] * 6,
            out_specs=VMEM,
            compiler_params=params(4),
            cost_estimate=cost(4 * out_weight.size, 0),
        )(wide, piece0, piece1, piece2, piece3, piece4)

    others = [partner(part, "ctx", k) for k, part in zip(far, parts)]
    core = near(1)
    others.append(partner(core, "ctx", 1))
    total = near(0)
    for other in others:
        total = total + other
    return total.astype(BF)


def solution(mesh):
    placed = (
        P(("groups", "beam"), "ctx"),
        P(("groups", "beam"), None),
        P(("groups", "beam"), None),
        P(("groups", "beam"), "ctx", None, None),
        P(("groups", "beam"), "ctx", None, None),
        P("groups"),
        P("groups"),
        P("ctx", "beam"),
    )
    return jax.shard_map(
        step,
        mesh=mesh,
        in_specs=placed,
        out_specs=P("groups", ("beam", "ctx")),
        check_vma=False,
    )
```

```python
import math

import jax
import jax.numpy as jnp
from jax import lax
from jax.experimental import pallas as pl
from jax.experimental.pallas import tpu as pltpu
from jax.sharding import PartitionSpec as P


H = 128
KVH = 8
HD = 128
SPAN = 128
GROUP = H // KVH

MASKED = -1e30
SCALE = 1.0 / math.sqrt(HD)

BF = jnp.bfloat16
F32 = jnp.float32
VMEM = pl.BlockSpec(memory_space=pltpu.VMEM)
HBM = pl.BlockSpec(memory_space=pltpu.HBM)
SHARES = (4, 5, 5, 5, 10, 3)


def params(mib):
    return pltpu.CompilerParams(vmem_limit_bytes=mib << 20)


def cost(flops, moved):
    return pl.CostEstimate(flops=flops, bytes_accessed=moved, transcendentals=0)


def partner(array, axis, k):
    return lax.ppermute(array, axis, [(i, i ^ k) for i in range(lax.axis_size(axis))])


def partners(arrays, axis):
    each = isinstance(arrays, (list, tuple))
    return [partner(arrays[k] if each else arrays, axis, k) for k in range(1, lax.axis_size(axis))]


def pack_kernel(heads, kv_count, q_hbm, k_hbm, v_hbm, out_ref, q_ref, k_ref, v_ref, rows, sems):
    copies = [
        pltpu.make_async_copy(src, dst, sems.at[n])
        for n, (src, dst) in enumerate(((q_hbm, q_ref), (k_hbm, k_ref), (v_hbm, v_ref)))
    ]
    for copy in copies:
        copy.start()
    start = lax.axis_index("ctx") * heads // GROUP
    rows[...] = jnp.zeros_like(rows)
    for copy in copies:
        copy.wait()
    for h in range(heads):
        rows[h : h + 1, :] = q_ref[:, h * HD : (h + 1) * HD].astype(F32)
    for r in range(kv_count):
        here = pl.ds(pl.multiple_of((start + r) * HD, HD), HD)
        rows[heads + r : heads + r + 1, :] = k_ref[:, here].astype(F32)
        rows[heads + kv_count + r : heads + kv_count + r + 1, :] = v_ref[:, here].astype(F32)
    out_ref[...] = rows[...].astype(BF)


def fetch_kernel(start, w_hbm, out_ref, sem):
    copy = pltpu.make_async_copy(w_hbm.at[pl.ds(start, out_ref.shape[0])], out_ref, sem)
    copy.start()
    copy.wait()


def relayout_kernel(start, k_hbm, v_hbm, w_hbm, kt, vt, piece, k_ref, v_ref, sems):
    copies = [
        pltpu.make_async_copy(src, dst, sems.at[n])
        for n, (src, dst) in enumerate(
            ((k_hbm, k_ref), (v_hbm, v_ref), (w_hbm.at[pl.ds(start, piece.shape[0])], piece))
        )
    ]
    for copy in copies:
        copy.start()
    copies[0].wait()
    kt[...] = pltpu.einshape("tkd->ktd", k_ref[0])
    copies[1].wait()
    vt[...] = pltpu.einshape("tkd->ktd", v_ref[0])
    copies[2].wait()


def stack_kernel(*refs):
    for n, ref in enumerate(refs[:-1]):
        refs[-1][n] = ref[...]


def split3(x):
    a = x.astype(BF)
    rest = x - a.astype(F32)
    b = rest.astype(BF)
    c = (rest - b.astype(F32)).astype(BF)
    return a, b, c


def eye(rows):
    shape = (rows, HD)
    return lax.broadcasted_iota(jnp.int32, shape, 0) == lax.broadcasted_iota(jnp.int32, shape, 1)


def attend_kernel(slots, start, beams, heads, kv_count, per_kv, tokens, *refs):
    n = len(slots)
    lengths_hbm, parents_hbm, w_hbm, kt, vt = refs[:5]
    stacks, outs = refs[5 : 5 + n], refs[5 + n : 5 + 2 * n]
    piece, lengths, parents, sems = refs[5 + 2 * n :]
    small = [
        pltpu.make_async_copy(lengths_hbm, lengths, sems.at[0]),
        pltpu.make_async_copy(parents_hbm, parents, sems.at[1]),
    ]
    large = pltpu.make_async_copy(w_hbm.at[pl.ds(start, piece.shape[0])], piece, sems.at[2])
    for copy in small:
        copy.start()
    large.start()
    b = lax.axis_index("beam")
    c = lax.axis_index("ctx")
    rows = beams * per_kv
    count = kv_count * rows
    pairs = [(i, r) for i in range(n) for r in range(kv_count)]

    def kv_head(i, r):
        return (c ^ slots[i]) * heads // GROUP + r

    scores = []
    for i, r in pairs:
        q = stacks[i][:, r * per_kv : (r + 1) * per_kv, :].astype(F32)
        q = q.reshape(rows, HD).astype(BF)
        scores.append(
            lax.dot_general(q, kt[kv_head(i, r)], (((1,), (1,)), ((), ())), preferred_element_type=F32)
        )
    for copy in small:
        copy.wait()
    limit = lengths[b] * SPAN - c * tokens
    keep = lax.broadcasted_iota(jnp.int32, (rows, tokens), 1) < limit
    scores = [jnp.where(keep, s * SCALE, MASKED) for s in scores]
    peaks = [jnp.max(s, axis=-1, keepdims=True) for s in scores]
    weights = [jnp.where(keep, jnp.exp(s - m), 0.0) for s, m in zip(scores, peaks)]
    totals = [jnp.sum(w, axis=-1, keepdims=True) for w in weights]
    blended = [
        jnp.dot(w.astype(BF), vt[kv_head(i, r)], preferred_element_type=F32)
        for w, (i, r) in zip(weights, pairs)
    ]
    safe = [jnp.where(t > 0.0, t, 1.0) for t in totals]
    lses = [jnp.where(t > 0.0, m + jnp.log(f), MASKED) for t, m, f in zip(totals, peaks, safe)]
    which = lax.broadcasted_iota(jnp.int32, (16, HD), 0)
    diagonal = eye(count)
    for i in range(n):
        mine = slice(i * kv_count, (i + 1) * kv_count)
        outs[i][0:count, :] = jnp.concatenate(
            [(o / f).astype(BF) for o, f in zip(blended[mine], safe[mine])], axis=0
        )
        lse = jnp.concatenate(lses[mine], axis=0)
        line = jnp.sum(jnp.where(diagonal, lse, 0.0), axis=0, keepdims=True)
        parts = [p.astype(F32) for p in split3(line)]
        stats = jnp.where(which == 0, parts[0], jnp.where(which == 1, parts[1], jnp.where(which == 2, parts[2], 0.0)))
        if slots[i] == 0:
            child = lax.broadcasted_iota(jnp.int32, (16, HD), 1) % rows // per_kv
            for k in range(beams):
                stats = jnp.where((which == 3) & (child == k) & (parents[b ^ k] == b), 1.0, stats)
        outs[i][count : count + 16, :] = stats.astype(BF)
    large.wait()


def merge_kernel(ctx_count, beams, heads, kv_count, per_kv, *refs):
    stack, states, out_ref = refs[0], refs[1 : 1 + ctx_count], refs[1 + ctx_count]
    b = lax.axis_index("beam")
    rows = beams * per_kv
    count = kv_count * rows
    diagonal = eye(count)
    own, value = [], []
    for r in range(kv_count):
        q = stack[:, r * per_kv : (r + 1) * per_kv, :].astype(F32)
        key = stack[:, heads + r : heads + r + 1, :].astype(F32)
        own.append(jnp.sum(q * key, axis=-1, keepdims=True).reshape(rows, 1) * SCALE)
        v = stack[:, heads + kv_count + r : heads + kv_count + r + 1, :].astype(F32)
        value.append(jnp.broadcast_to(v, (beams, per_kv, HD)).reshape(rows, HD))
    own = jnp.concatenate(own, axis=0) if kv_count > 1 else own[0]
    value = jnp.concatenate(value, axis=0) if kv_count > 1 else value[0]
    lses = []
    for k in range(ctx_count):
        line = states[k][count : count + 16, :].astype(F32)
        if k == 0:
            mine = jnp.sum(jnp.where(diagonal, line[3:4], 0.0), axis=-1, keepdims=True)
        line = line[0:1] + line[1:2] + line[2:3]
        lses.append(jnp.sum(jnp.where(diagonal, line, 0.0), axis=-1, keepdims=True))
    peak = own
    for lse in lses:
        peak = jnp.maximum(peak, lse)
    weight = jnp.exp(own - peak)
    total = weight
    blended = weight * value
    for k in range(ctx_count):
        weight = jnp.exp(lses[k] - peak)
        total = total + weight
        blended = blended + weight * states[k][0:count, :].astype(F32)
    result = jnp.where(mine > 0.0, blended / total, 0.0).astype(BF)
    for r in range(kv_count):
        for i in range(beams):
            at = r * rows + i * per_kv
            out_ref[b ^ i, r * per_kv : (r + 1) * per_kv, :] = result[at : at + per_kv, :]


def chunk(rows, pieces, bounds, beams, at, width):
    return sum(
        jnp.dot(rows[:, lo:hi], ref[:, pl.ds(at, width)], preferred_element_type=F32)
        for ref, lo, hi in zip(pieces, bounds, bounds[1:])
    )[:beams]


def project_kernel(ctx_count, far, beams, heads, bounds, *refs):
    held = len(bounds) - 2
    rows_of, pieces, w_hbm = refs[:beams], refs[beams : beams + held], refs[beams + held]
    outs, (last, wide), (laid, sem) = refs[beams + held + 1 : -4], refs[-4:-2], refs[-2:]
    copy = pltpu.make_async_copy(w_hbm.at[pl.ds(bounds[held], last.shape[0])], last, sem)
    copy.start()
    c = lax.axis_index("ctx")
    laid[...] = jnp.zeros_like(laid)
    for i in range(beams):
        row = rows_of[0][i].astype(F32)
        for k in range(1, beams):
            row = row + rows_of[k][i].astype(F32)
        laid[i * heads : (i + 1) * heads, :] = row
    for h in range(heads):
        wide[:, h * HD : (h + 1) * HD] = laid[pl.ds(h, 8, stride=heads), :].astype(BF)
    columns = last.shape[1] // ctx_count
    width = min(512, columns)
    places = [(n, k, j) for n, k in enumerate(far) for j in range(0, columns, width)]
    for n, k, j in places:
        at = pl.multiple_of((c ^ k) * columns + j, 128)
        outs[n][:, j : j + width] = chunk(wide, pieces, bounds[: held + 1], beams, at, width)
    copy.wait()
    for n, k, j in places:
        at = pl.multiple_of((c ^ k) * columns + j, 128)
        outs[n][:, j : j + width] += chunk(wide, [last], bounds[held:], beams, at, width)


def near_kernel(ctx_count, k, beams, bounds, wide, *refs):
    pieces, out_ref = refs[:-1], refs[-1]
    columns = pieces[0].shape[1] // ctx_count
    width = min(512, columns)
    for j in range(0, columns, width):
        at = pl.multiple_of((lax.axis_index("ctx") ^ k) * columns + j, 128)
        out_ref[:, j : j + width] = chunk(wide, pieces, bounds, beams, at, width)


def step(queries, new_keys, new_values, cache_keys, cache_values, parents, lengths, out_weight):
    ctx_count = lax.axis_size("ctx")
    beams = lax.axis_size("beam")
    heads = queries.shape[1] // HD
    tokens = cache_keys.shape[1]
    kv_count = max(1, heads // GROUP)
    per_kv = min(heads, GROUP)
    packet_rows = -(-(heads + 2 * kv_count) // 16) * 16
    count = beams * heads

    queries, new_keys, new_values, parents, lengths, out_weight = (
        pltpu.with_memory_space_constraint(x, pltpu.HBM)
        for x in (queries, new_keys, new_values, parents, lengths, out_weight)
    )
    cache_keys = pltpu.with_memory_space_constraint(cache_keys, pltpu.HBM)
    cache_values = pltpu.with_memory_space_constraint(cache_values, pltpu.HBM)
    bounds = [round(heads * sum(SHARES[:n]) / sum(SHARES)) * HD for n in range(len(SHARES) + 1)]
    piece = [jax.ShapeDtypeStruct((hi - lo, out_weight.shape[1]), BF) for lo, hi in zip(bounds, bounds[1:])]

    def fetch(n):
        return pl.pallas_call(
            lambda *refs: fetch_kernel(bounds[n], *refs),
            out_shape=piece[n],
            in_specs=[HBM],
            out_specs=VMEM,
            scratch_shapes=[pltpu.SemaphoreType.DMA],
            compiler_params=params(4),
            cost_estimate=cost(0, 2 * piece[n].size),
        )(out_weight)

    def attend(slots, n):
        return pl.pallas_call(
            lambda *refs: attend_kernel(slots, bounds[n], beams, heads, kv_count, per_kv, tokens, *refs),
            out_shape=[jax.ShapeDtypeStruct((count + 16, HD), BF)] * len(slots) + [piece[n]],
            in_specs=[HBM] * 3 + [VMEM] * (len(slots) + 2),
            out_specs=[VMEM] * (len(slots) + 1),
            scratch_shapes=[pltpu.SMEM(lengths.shape, jnp.int32)] * 2 + [pltpu.SemaphoreType.DMA((3,))],
            compiler_params=params(12),
            cost_estimate=cost(4 * count * len(slots) * tokens * HD, 2 * piece[n].size),
        )(lengths, parents, out_weight, kt, vt, *[stacks[k] for k in slots])

    packet = pl.pallas_call(
        lambda *refs: pack_kernel(heads, kv_count, *refs),
        out_shape=jax.ShapeDtypeStruct((packet_rows, HD), BF),
        in_specs=[HBM] * 3,
        out_specs=VMEM,
        scratch_shapes=[pltpu.VMEM(x.shape, BF) for x in (queries, new_keys, new_values)]
        + [pltpu.VMEM((packet_rows, HD), F32), pltpu.SemaphoreType.DMA((3,))],
        compiler_params=params(4),
        name="pack",
    )(queries, new_keys, new_values)
    turned = jax.ShapeDtypeStruct((KVH, tokens, HD), BF)
    kt, vt, piece0 = pl.pallas_call(
        lambda *refs: relayout_kernel(bounds[0], *refs),
        out_shape=[turned, turned, piece[0]],
        in_specs=[HBM] * 3,
        out_specs=[VMEM] * 3,
        scratch_shapes=[pltpu.VMEM(cache_keys.shape, BF)] * 2 + [pltpu.SemaphoreType.DMA((3,))],
        compiler_params=params(8),
        cost_estimate=cost(0, 4 * turned.size + 2 * piece[0].size),
        name="relayout",
    )(cache_keys, cache_values, out_weight)
    packets = [packet] + partners(packet, "beam")
    stack = pl.pallas_call(
        stack_kernel,
        out_shape=jax.ShapeDtypeStruct((beams,) + packet.shape, BF),
        in_specs=[VMEM] * beams,
        out_specs=VMEM,
        compiler_params=params(4),
        name="stack",
    )(*packets)
    stacks = [stack] + partners(stack, "ctx")
    own_state, piece1 = attend((0,), 1)
    *states, piece2 = attend(tuple(range(1, ctx_count)), 2)
    states = [own_state] + partners([None] + states, "ctx")
    piece3 = fetch(3)

    attended = pl.pallas_call(
        lambda *refs: merge_kernel(ctx_count, beams, heads, kv_count, per_kv, *refs),
        out_shape=jax.ShapeDtypeStruct((beams, heads, HD), BF),
        in_specs=[VMEM] * (1 + ctx_count),
        out_specs=VMEM,
        compiler_params=params(8),
        name="merge",
    )(stack, *states)
    rows_of = [attended] + partners(attended, "beam")

    piece4 = fetch(4)
    held = (piece0, piece1, piece2, piece3, piece4)

    columns = out_weight.shape[1] // ctx_count
    part = jax.ShapeDtypeStruct((beams, columns), F32)
    wide = jax.ShapeDtypeStruct((8, heads * HD), BF)
    far = tuple(range(2, ctx_count))
    *parts, piece5, wide = pl.pallas_call(
        lambda *refs: project_kernel(ctx_count, far, beams, heads, bounds, *refs),
        out_shape=[part] * len(far) + [piece[5], wide],
        in_specs=[VMEM] * (beams + len(held)) + [HBM],
        out_specs=[VMEM] * (len(far) + 2),
        scratch_shapes=[pltpu.VMEM((8 * heads, HD), F32), pltpu.SemaphoreType.DMA],
        compiler_params=params(8),
        cost_estimate=cost(8 * out_weight.size, 2 * piece[5].size),
        name="project",
    )(*rows_of, *held, out_weight)

    def near(k):
        return pl.pallas_call(
            lambda *refs: near_kernel(ctx_count, k, beams, bounds, *refs),
            out_shape=part,
            in_specs=[VMEM] * (len(held) + 2),
            out_specs=VMEM,
            compiler_params=params(4),
            cost_estimate=cost(4 * out_weight.size, 0),
        )(wide, *held, piece5)

    others = [partner(part, "ctx", k) for k, part in zip(far, parts)]
    core = near(1)
    others.append(partner(core, "ctx", 1))
    total = near(0)
    for other in others:
        total = total + other
    return total.astype(BF)


def solution(mesh):
    placed = (
        P(("groups", "beam"), "ctx"),
        P(("groups", "beam"), None),
        P(("groups", "beam"), None),
        P(("groups", "beam"), "ctx", None, None),
        P(("groups", "beam"), "ctx", None, None),
        P("groups"),
        P("groups"),
        P("ctx", "beam"),
    )
    return jax.shard_map(
        step,
        mesh=mesh,
        in_specs=placed,
        out_specs=P("groups", ("beam", "ctx")),
        check_vma=False,
    )
```

```python
import math

import jax
import jax.numpy as jnp
from jax import lax
from jax.experimental import pallas as pl
from jax.experimental.pallas import tpu as pltpu
from jax.sharding import PartitionSpec as P


H = 128
KVH = 8
HD = 128
SPAN = 128
GROUP = H // KVH

MASKED = -1e30
SCALE = 1.0 / math.sqrt(HD)

BF = jnp.bfloat16
F32 = jnp.float32
VMEM = pl.BlockSpec(memory_space=pltpu.VMEM)
HBM = pl.BlockSpec(memory_space=pltpu.HBM)
SHARES = (4, 5, 5, 6, 10, 2)


def params(mib):
    return pltpu.CompilerParams(vmem_limit_bytes=mib << 20)


def cost(flops, moved):
    return pl.CostEstimate(flops=flops, bytes_accessed=moved, transcendentals=0)


def partner(array, axis, k):
    return lax.ppermute(array, axis, [(i, i ^ k) for i in range(lax.axis_size(axis))])


def partners(arrays, axis):
    each = isinstance(arrays, (list, tuple))
    return [partner(arrays[k] if each else arrays, axis, k) for k in range(1, lax.axis_size(axis))]


def pack_kernel(heads, kv_count, q_hbm, k_hbm, v_hbm, out_ref, q_ref, k_ref, v_ref, rows, sems):
    copies = [
        pltpu.make_async_copy(src, dst, sems.at[n])
        for n, (src, dst) in enumerate(((q_hbm, q_ref), (k_hbm, k_ref), (v_hbm, v_ref)))
    ]
    for copy in copies:
        copy.start()
    start = lax.axis_index("ctx") * heads // GROUP
    rows[...] = jnp.zeros_like(rows)
    for copy in copies:
        copy.wait()
    for h in range(heads):
        rows[h : h + 1, :] = q_ref[:, h * HD : (h + 1) * HD].astype(F32)
    for r in range(kv_count):
        here = pl.ds(pl.multiple_of((start + r) * HD, HD), HD)
        rows[heads + r : heads + r + 1, :] = k_ref[:, here].astype(F32)
        rows[heads + kv_count + r : heads + kv_count + r + 1, :] = v_ref[:, here].astype(F32)
    out_ref[...] = rows[...].astype(BF)


def fetch_kernel(start, w_hbm, out_ref, sem):
    copy = pltpu.make_async_copy(w_hbm.at[pl.ds(start, out_ref.shape[0])], out_ref, sem)
    copy.start()
    copy.wait()


def relayout_kernel(start, k_hbm, v_hbm, w_hbm, kt, vt, piece, k_ref, v_ref, sems):
    copies = [
        pltpu.make_async_copy(src, dst, sems.at[n])
        for n, (src, dst) in enumerate(
            ((k_hbm, k_ref), (v_hbm, v_ref), (w_hbm.at[pl.ds(start, piece.shape[0])], piece))
        )
    ]
    for copy in copies:
        copy.start()
    copies[0].wait()
    kt[...] = pltpu.einshape("tkd->ktd", k_ref[0])
    copies[1].wait()
    vt[...] = pltpu.einshape("tkd->ktd", v_ref[0])
    copies[2].wait()


def stack_kernel(*refs):
    for n, ref in enumerate(refs[:-1]):
        refs[-1][n] = ref[...]


def split3(x):
    a = x.astype(BF)
    rest = x - a.astype(F32)
    b = rest.astype(BF)
    c = (rest - b.astype(F32)).astype(BF)
    return a, b, c


def eye(rows):
    shape = (rows, HD)
    return lax.broadcasted_iota(jnp.int32, shape, 0) == lax.broadcasted_iota(jnp.int32, shape, 1)


def attend_kernel(slots, start, beams, heads, kv_count, per_kv, tokens, *refs):
    n = len(slots)
    lengths_hbm, parents_hbm, w_hbm, kt, vt = refs[:5]
    stacks, outs = refs[5 : 5 + n], refs[5 + n : 5 + 2 * n]
    piece, lengths, parents, sems = refs[5 + 2 * n :]
    small = [
        pltpu.make_async_copy(lengths_hbm, lengths, sems.at[0]),
        pltpu.make_async_copy(parents_hbm, parents, sems.at[1]),
    ]
    large = pltpu.make_async_copy(w_hbm.at[pl.ds(start, piece.shape[0])], piece, sems.at[2])
    for copy in small:
        copy.start()
    large.start()
    b = lax.axis_index("beam")
    c = lax.axis_index("ctx")
    rows = beams * per_kv
    count = kv_count * rows
    pairs = [(i, r) for i in range(n) for r in range(kv_count)]

    def kv_head(i, r):
        return (c ^ slots[i]) * heads // GROUP + r

    scores = []
    for i, r in pairs:
        q = stacks[i][:, r * per_kv : (r + 1) * per_kv, :].astype(F32)
        q = q.reshape(rows, HD).astype(BF)
        scores.append(
            lax.dot_general(q, kt[kv_head(i, r)], (((1,), (1,)), ((), ())), preferred_element_type=F32)
        )
    for copy in small:
        copy.wait()
    limit = lengths[b] * SPAN - c * tokens
    keep = lax.broadcasted_iota(jnp.int32, (rows, tokens), 1) < limit
    scores = [jnp.where(keep, s * SCALE, MASKED) for s in scores]
    peaks = [jnp.max(s, axis=-1, keepdims=True) for s in scores]
    weights = [jnp.where(keep, jnp.exp(s - m), 0.0) for s, m in zip(scores, peaks)]
    totals = [jnp.sum(w, axis=-1, keepdims=True) for w in weights]
    blended = [
        jnp.dot(w.astype(BF), vt[kv_head(i, r)], preferred_element_type=F32)
        for w, (i, r) in zip(weights, pairs)
    ]
    safe = [jnp.where(t > 0.0, t, 1.0) for t in totals]
    lses = [jnp.where(t > 0.0, m + jnp.log(f), MASKED) for t, m, f in zip(totals, peaks, safe)]
    which = lax.broadcasted_iota(jnp.int32, (16, HD), 0)
    diagonal = eye(count)
    for i in range(n):
        mine = slice(i * kv_count, (i + 1) * kv_count)
        outs[i][0:count, :] = jnp.concatenate(
            [(o / f).astype(BF) for o, f in zip(blended[mine], safe[mine])], axis=0
        )
        lse = jnp.concatenate(lses[mine], axis=0)
        line = jnp.sum(jnp.where(diagonal, lse, 0.0), axis=0, keepdims=True)
        parts = [p.astype(F32) for p in split3(line)]
        stats = jnp.where(which == 0, parts[0], jnp.where(which == 1, parts[1], jnp.where(which == 2, parts[2], 0.0)))
        if slots[i] == 0:
            child = lax.broadcasted_iota(jnp.int32, (16, HD), 1) % rows // per_kv
            for k in range(beams):
                stats = jnp.where((which == 3) & (child == k) & (parents[b ^ k] == b), 1.0, stats)
        outs[i][count : count + 16, :] = stats.astype(BF)
    large.wait()


def merge_kernel(ctx_count, beams, heads, kv_count, per_kv, *refs):
    stack, states, out_ref = refs[0], refs[1 : 1 + ctx_count], refs[1 + ctx_count]
    b = lax.axis_index("beam")
    rows = beams * per_kv
    count = kv_count * rows
    diagonal = eye(count)
    own, value = [], []
    for r in range(kv_count):
        q = stack[:, r * per_kv : (r + 1) * per_kv, :].astype(F32)
        key = stack[:, heads + r : heads + r + 1, :].astype(F32)
        own.append(jnp.sum(q * key, axis=-1, keepdims=True).reshape(rows, 1) * SCALE)
        v = stack[:, heads + kv_count + r : heads + kv_count + r + 1, :].astype(F32)
        value.append(jnp.broadcast_to(v, (beams, per_kv, HD)).reshape(rows, HD))
    own = jnp.concatenate(own, axis=0) if kv_count > 1 else own[0]
    value = jnp.concatenate(value, axis=0) if kv_count > 1 else value[0]
    lses = []
    for k in range(ctx_count):
        line = states[k][count : count + 16, :].astype(F32)
        if k == 0:
            mine = jnp.sum(jnp.where(diagonal, line[3:4], 0.0), axis=-1, keepdims=True)
        line = line[0:1] + line[1:2] + line[2:3]
        lses.append(jnp.sum(jnp.where(diagonal, line, 0.0), axis=-1, keepdims=True))
    peak = own
    for lse in lses:
        peak = jnp.maximum(peak, lse)
    weight = jnp.exp(own - peak)
    total = weight
    blended = weight * value
    for k in range(ctx_count):
        weight = jnp.exp(lses[k] - peak)
        total = total + weight
        blended = blended + weight * states[k][0:count, :].astype(F32)
    result = jnp.where(mine > 0.0, blended / total, 0.0).astype(BF)
    for r in range(kv_count):
        for i in range(beams):
            at = r * rows + i * per_kv
            out_ref[b ^ i, r * per_kv : (r + 1) * per_kv, :] = result[at : at + per_kv, :]


def chunk(rows, pieces, bounds, beams, at, width):
    return sum(
        jnp.dot(rows[:, lo:hi], ref[:, pl.ds(at, width)], preferred_element_type=F32)
        for ref, lo, hi in zip(pieces, bounds, bounds[1:])
    )[:beams]


def project_kernel(ctx_count, far, beams, heads, bounds, *refs):
    held = len(bounds) - 2
    rows_of, pieces, w_hbm = refs[:beams], refs[beams : beams + held], refs[beams + held]
    outs, (last, wide), (laid, sem) = refs[beams + held + 1 : -4], refs[-4:-2], refs[-2:]
    copy = pltpu.make_async_copy(w_hbm.at[pl.ds(bounds[held], last.shape[0])], last, sem)
    copy.start()
    c = lax.axis_index("ctx")
    laid[...] = jnp.zeros_like(laid)
    for i in range(beams):
        row = rows_of[0][i].astype(F32)
        for k in range(1, beams):
            row = row + rows_of[k][i].astype(F32)
        laid[i * heads : (i + 1) * heads, :] = row
    for h in range(heads):
        wide[:, h * HD : (h + 1) * HD] = laid[pl.ds(h, 8, stride=heads), :].astype(BF)
    columns = last.shape[1] // ctx_count
    width = min(512, columns)
    places = [(n, k, j) for n, k in enumerate(far) for j in range(0, columns, width)]
    for n, k, j in places:
        at = pl.multiple_of((c ^ k) * columns + j, 128)
        outs[n][:, j : j + width] = chunk(wide, pieces, bounds[: held + 1], beams, at, width)
    copy.wait()
    for n, k, j in places:
        at = pl.multiple_of((c ^ k) * columns + j, 128)
        outs[n][:, j : j + width] += chunk(wide, [last], bounds[held:], beams, at, width)


def near_kernel(ctx_count, k, beams, bounds, wide, *refs):
    pieces, out_ref = refs[:-1], refs[-1]
    columns = pieces[0].shape[1] // ctx_count
    width = min(512, columns)
    for j in range(0, columns, width):
        at = pl.multiple_of((lax.axis_index("ctx") ^ k) * columns + j, 128)
        out_ref[:, j : j + width] = chunk(wide, pieces, bounds, beams, at, width)


def step(queries, new_keys, new_values, cache_keys, cache_values, parents, lengths, out_weight):
    ctx_count = lax.axis_size("ctx")
    beams = lax.axis_size("beam")
    heads = queries.shape[1] // HD
    tokens = cache_keys.shape[1]
    kv_count = max(1, heads // GROUP)
    per_kv = min(heads, GROUP)
    packet_rows = -(-(heads + 2 * kv_count) // 16) * 16
    count = beams * heads

    queries, new_keys, new_values, parents, lengths, out_weight = (
        pltpu.with_memory_space_constraint(x, pltpu.HBM)
        for x in (queries, new_keys, new_values, parents, lengths, out_weight)
    )
    cache_keys = pltpu.with_memory_space_constraint(cache_keys, pltpu.HBM)
    cache_values = pltpu.with_memory_space_constraint(cache_values, pltpu.HBM)
    ends = [round(heads * sum(SHARES[:n]) / sum(SHARES)) for n in range(len(SHARES) + 1)]
    bounds = [min(end, heads - len(SHARES) + n) * HD for n, end in enumerate(ends)]
    piece = [jax.ShapeDtypeStruct((hi - lo, out_weight.shape[1]), BF) for lo, hi in zip(bounds, bounds[1:])]

    def fetch(n):
        return pl.pallas_call(
            lambda *refs: fetch_kernel(bounds[n], *refs),
            out_shape=piece[n],
            in_specs=[HBM],
            out_specs=VMEM,
            scratch_shapes=[pltpu.SemaphoreType.DMA],
            compiler_params=params(4),
            cost_estimate=cost(0, 2 * piece[n].size),
        )(out_weight)

    def attend(slots, n):
        return pl.pallas_call(
            lambda *refs: attend_kernel(slots, bounds[n], beams, heads, kv_count, per_kv, tokens, *refs),
            out_shape=[jax.ShapeDtypeStruct((count + 16, HD), BF)] * len(slots) + [piece[n]],
            in_specs=[HBM] * 3 + [VMEM] * (len(slots) + 2),
            out_specs=[VMEM] * (len(slots) + 1),
            scratch_shapes=[pltpu.SMEM(lengths.shape, jnp.int32)] * 2 + [pltpu.SemaphoreType.DMA((3,))],
            compiler_params=params(12),
            cost_estimate=cost(4 * count * len(slots) * tokens * HD, 2 * piece[n].size),
        )(lengths, parents, out_weight, kt, vt, *[stacks[k] for k in slots])

    packet = pl.pallas_call(
        lambda *refs: pack_kernel(heads, kv_count, *refs),
        out_shape=jax.ShapeDtypeStruct((packet_rows, HD), BF),
        in_specs=[HBM] * 3,
        out_specs=VMEM,
        scratch_shapes=[pltpu.VMEM(x.shape, BF) for x in (queries, new_keys, new_values)]
        + [pltpu.VMEM((packet_rows, HD), F32), pltpu.SemaphoreType.DMA((3,))],
        compiler_params=params(4),
        name="pack",
    )(queries, new_keys, new_values)
    turned = jax.ShapeDtypeStruct((KVH, tokens, HD), BF)
    kt, vt, piece0 = pl.pallas_call(
        lambda *refs: relayout_kernel(bounds[0], *refs),
        out_shape=[turned, turned, piece[0]],
        in_specs=[HBM] * 3,
        out_specs=[VMEM] * 3,
        scratch_shapes=[pltpu.VMEM(cache_keys.shape, BF)] * 2 + [pltpu.SemaphoreType.DMA((3,))],
        compiler_params=params(8),
        cost_estimate=cost(0, 4 * turned.size + 2 * piece[0].size),
        name="relayout",
    )(cache_keys, cache_values, out_weight)
    packets = [packet] + partners(packet, "beam")
    stack = pl.pallas_call(
        stack_kernel,
        out_shape=jax.ShapeDtypeStruct((beams,) + packet.shape, BF),
        in_specs=[VMEM] * beams,
        out_specs=VMEM,
        compiler_params=params(4),
        name="stack",
    )(*packets)
    stacks = [stack] + partners(stack, "ctx")
    own_state, piece1 = attend((0,), 1)
    *states, piece2 = attend(tuple(range(1, ctx_count)), 2)
    states = [own_state] + partners([None] + states, "ctx")
    piece3 = fetch(3)

    attended = pl.pallas_call(
        lambda *refs: merge_kernel(ctx_count, beams, heads, kv_count, per_kv, *refs),
        out_shape=jax.ShapeDtypeStruct((beams, heads, HD), BF),
        in_specs=[VMEM] * (1 + ctx_count),
        out_specs=VMEM,
        compiler_params=params(8),
        name="merge",
    )(stack, *states)
    rows_of = [attended] + partners(attended, "beam")

    piece4 = fetch(4)
    held = (piece0, piece1, piece2, piece3, piece4)

    columns = out_weight.shape[1] // ctx_count
    part = jax.ShapeDtypeStruct((beams, columns), F32)
    wide = jax.ShapeDtypeStruct((8, heads * HD), BF)
    far = tuple(range(2, ctx_count))
    *parts, piece5, wide = pl.pallas_call(
        lambda *refs: project_kernel(ctx_count, far, beams, heads, bounds, *refs),
        out_shape=[part] * len(far) + [piece[5], wide],
        in_specs=[VMEM] * (beams + len(held)) + [HBM],
        out_specs=[VMEM] * (len(far) + 2),
        scratch_shapes=[pltpu.VMEM((8 * heads, HD), F32), pltpu.SemaphoreType.DMA],
        compiler_params=params(8),
        cost_estimate=cost(8 * out_weight.size, 2 * piece[5].size),
        name="project",
    )(*rows_of, *held, out_weight)

    def near(k):
        return pl.pallas_call(
            lambda *refs: near_kernel(ctx_count, k, beams, bounds, *refs),
            out_shape=part,
            in_specs=[VMEM] * (len(held) + 2),
            out_specs=VMEM,
            compiler_params=params(4),
            cost_estimate=cost(4 * out_weight.size, 0),
        )(wide, *held, piece5)

    others = [partner(part, "ctx", k) for k, part in zip(far, parts)]
    core = near(1)
    others.append(partner(core, "ctx", 1))
    total = near(0)
    for other in others:
        total = total + other
    return total.astype(BF)


def solution(mesh):
    placed = (
        P(("groups", "beam"), "ctx"),
        P(("groups", "beam"), None),
        P(("groups", "beam"), None),
        P(("groups", "beam"), "ctx", None, None),
        P(("groups", "beam"), "ctx", None, None),
        P("groups"),
        P("groups"),
        P("ctx", "beam"),
    )
    return jax.shard_map(
        step,
        mesh=mesh,
        in_specs=placed,
        out_specs=P("groups", ("beam", "ctx")),
        check_vma=False,
    )
```
